768 devices in a mesh: dp: 4 (over x), pipe: 12 (over z), ctx: 16 (over y, core).
Axes of the slice: x: 4, y: 8, z: 12, core: 2. Of those that a mesh axis runs over, the one named last changes fastest.
Arguments:
- ssm_input: bfloat16 [4, 12, 4096, 1024], P('dp', 'pipe', 'ctx'), may hold values from -6 to 6
- state_write: bfloat16 [4, 12, 4096, 128], P('dp', 'pipe', 'ctx'), may hold values from -0.1875 to 0.1875
- state_read: bfloat16 [4, 12, 4096, 128], P('dp', 'pipe', 'ctx'), may hold values from -0.1875 to 0.1875
- step_raw: bfloat16 [4, 12, 4096, 16], P('dp', 'pipe', 'ctx'), may hold values from -6 to 6
- decay_log: float32 [12, 16], P('pipe'), may hold values from -20 to -3
- step_bias: float32 [12, 16], P('pipe'), may hold values from -1 to 1
- skip_gain: float32 [12, 16], P('pipe'), may hold values from 0.5 to 1.5
- out_grad: bfloat16 [4, 12, 4096, 1024], P('dp', 'pipe', 'ctx'), may hold values from -6 to 6
Outputs:
- ssm_output: bfloat16 [4, 12, 4096, 1024], P('dp', 'pipe', 'ctx')
- prev_grad_x: bfloat16 [4, 12, 4096, 1024], P('dp', 'pipe', 'ctx')
- prev_grad_write: bfloat16 [4, 12, 4096, 128], P('dp', 'pipe', 'ctx')
- prev_grad_read: bfloat16 [4, 12, 4096, 128], P('dp', 'pipe', 'ctx')
- prev_grad_step: bfloat16 [4, 12, 4096, 16], P('dp', 'pipe', 'ctx')
- param_grads: float32 [12, 3, 16], P('pipe')
The draws below stay inside these ranges and needn't reach their ends.
All inputs are finite; a program needn't handle non-finite values.
Results may differ from the reference program's by a relative error of at most 0.008.
Values may be sent and summed in bfloat16 or wider, within the bound.
No kernel may reach another device: no remote copies, remote signals or barrier semaphores. Data moves between devices by JAX's collectives and lax.ppermute only.
A program may use at most 64 MiB of HBM per device.

```python
import jax
import jax.numpy as jnp
from jax import lax

HEAD_DIM = 64
STATE = 128
HEADS = 16
BLOCK = 256
WIDTH = 1024
SEQ = 4096
SECTIONS = 12
REPLICAS = 4


def draw_decay_log(key, part):
    low_end = jnp.log(1.0 / SEQ)
    high_end = jnp.log(0.04)
    fraction = jax.random.uniform(key, (SECTIONS, HEADS), jnp.float32)
    return (low_end + (high_end - low_end) * fraction).astype(jnp.float32)


def steps_of(own_key, dims, shards, least, largest):
    def one(position, shards_of):
        draws = jax.random.uniform(jax.random.fold_in(jax.random.fold_in(own_key, 6), position), (shards_of,), jnp.float32, least / len(shards), largest / len(shards))
        return jnp.repeat(jnp.exp(draws), dims[position] // shards_of).reshape((-1,) + (1,) * (len(dims) - position - 1))

    gain = one(*shards[0])
    for cut in shards[1:]:
        gain = gain * one(*cut)
    return gain


def noise(stream_key, shape, deviation, reach, cuts=(), dtype=jnp.bfloat16):
    level = steps_of(stream_key, shape, cuts, -0.22, 0.18) if cuts else 1.0
    result = jax.random.normal(stream_key, shape, jnp.float32) * deviation * level
    return jnp.minimum(jnp.maximum(result, -reach), reach).astype(dtype)


def setup_inputs(seed: int = 0) -> dict:
    key_of = jax.random.split(jax.random.key(seed), 9)
    return {
        "ssm_input": noise(key_of[0], (REPLICAS, SECTIONS, SEQ, WIDTH), 1.0, 6.0, ((0, 4), (1, 12), (2, 16))),
        "state_write": noise(key_of[1], (REPLICAS, SECTIONS, SEQ, STATE), (0.8 * (STATE * SEQ) ** -0.25), 0.1875, ((0, 4), (1, 12), (2, 16))),
        "state_read": noise(key_of[2], (REPLICAS, SECTIONS, SEQ, STATE), (0.8 * (STATE * SEQ) ** -0.25), 0.1875, ((0, 4), (1, 12), (2, 16))),
        "step_raw": noise(key_of[3], (REPLICAS, SECTIONS, SEQ, HEADS), 1.0, 6.0, ((0, 4), (1, 12), (2, 16))),
        "decay_log": draw_decay_log(jax.random.fold_in(key_of[8], 71), 0),
        "step_bias": jnp.clip(jax.random.uniform(key_of[5], (SECTIONS, HEADS), jnp.float32, -1.0, 1.0) * steps_of(key_of[5], (SECTIONS, HEADS), ((0, 12),), -0.4, 0.0), -1.0, 1.0),
        "skip_gain": jnp.clip(0.5 + 1.0 * jax.random.uniform(key_of[6], (SECTIONS, HEADS), jnp.float32) ** steps_of(key_of[6], (SECTIONS, HEADS), ((0, 12),), -0.2, 0.2), 0.5, 1.5),
        "out_grad": noise(key_of[7], (REPLICAS, SECTIONS, SEQ, WIDTH), 1.0, 6.0, ((0, 4), (1, 12), (2, 16))),
    }


def layer_scan(features, write_rows, read_rows, raw_step, log_rate, bias_step, gain_row, initial):
    length, head_count, head_dim = features.shape
    blocks = length // BLOCK
    step_size = jax.nn.softplus(raw_step.astype(jnp.float32) + bias_step)
    rate_all = step_size * -jnp.exp(log_rate)
    step_blocks = step_size.reshape(blocks, BLOCK, head_count)
    running = jnp.cumsum(rate_all.reshape(blocks, BLOCK, head_count), axis=1)
    feat_blocks = features.reshape(blocks, BLOCK, head_count, head_dim)
    write_blocks = write_rows.reshape(blocks, BLOCK, -1)
    read_blocks = read_rows.reshape(blocks, BLOCK, -1)
    scores = jnp.einsum('kqn,ksn->kqs', read_blocks, write_blocks, precision=lax.Precision.HIGHEST)
    by_head = jnp.swapaxes(running, 1, 2)
    spread = by_head[:, :, :, None] - by_head[:, :, None, :]
    row_index = lax.broadcasted_iota(jnp.int32, (BLOCK, BLOCK), 0)
    column_index = lax.broadcasted_iota(jnp.int32, (BLOCK, BLOCK), 1)
    causal = row_index >= column_index
    decays = jnp.exp(jnp.where(causal, spread, -jnp.inf))
    weights = (scores[:, None] * decays * jnp.swapaxes(step_blocks, 1, 2)[:, :, None, :]).astype(jnp.bfloat16)
    within = jnp.einsum('khts,kshp->kthp', weights.astype(jnp.float32), feat_blocks, precision=lax.Precision.HIGHEST)
    tail_scale = jnp.exp(running[:, -1:, :] - running) * step_blocks
    pieces = jnp.einsum('ksn,kshp->khnp', write_blocks, feat_blocks * tail_scale[..., None], precision=lax.Precision.HIGHEST)
    block_drop = jnp.exp(running[:, -1, :])

    def advance(carry_state, entries):
        block_piece, drop_now = entries
        return (drop_now[:, None, None] * carry_state + block_piece, carry_state)
    final_state, starts = lax.scan(advance, initial, (pieces, block_drop))
    carried = jnp.einsum('kqn,khnp->kqhp', read_blocks, starts, precision=lax.Precision.HIGHEST) * jnp.exp(running)[..., None]
    summed = within + carried + gain_row[None, None, :, None] * feat_blocks
    return (summed.reshape(length, head_count, head_dim).astype(jnp.bfloat16), final_state)

def reference(ssm_input, state_write, state_read, step_raw, decay_log, step_bias, skip_gain, out_grad):
    replicas = ssm_input.shape[0]
    sections = ssm_input.shape[1]
    pairs = replicas * sections

    def flatten(array):
        return array.reshape((pairs,) + array.shape[2:])

    def per_section(array):
        return jnp.broadcast_to(array[None], (replicas,) + array.shape).reshape((pairs,) + array.shape[1:])

    def single(entries):
        feat_in, write_in, read_in, step_in, log_in, bias_in, gain_in, grad_in = entries
        initial = jnp.zeros((HEADS, STATE, HEAD_DIM), jnp.float32)

        def forward(features, write_rows, read_rows, raw_step, log_rate, bias_step, gain_row):
            return layer_scan(features, write_rows, read_rows, raw_step, log_rate, bias_step, gain_row, initial)
        outputs, pullback = jax.vjp(forward, feat_in.reshape(SEQ, HEADS, HEAD_DIM).astype(jnp.float32), write_in.astype(jnp.float32), read_in.astype(jnp.float32), step_in, log_in, bias_in, gain_in)
        gradients = pullback((grad_in.reshape(SEQ, HEADS, HEAD_DIM), jnp.zeros_like(outputs[1])))
        return (outputs[0].reshape(SEQ, WIDTH), gradients[0].reshape(SEQ, WIDTH).astype(jnp.bfloat16), gradients[1].astype(jnp.bfloat16), gradients[2].astype(jnp.bfloat16), gradients[3], jnp.stack([gradients[4], gradients[5], gradients[6]]))
    results = lax.map(single, (flatten(ssm_input), flatten(state_write), flatten(state_read), flatten(step_raw), per_section(decay_log), per_section(step_bias), per_section(skip_gain), flatten(out_grad)))

    def onward(array):
        shaped = array.reshape((replicas, sections) + array.shape[1:])
        return jnp.concatenate([shaped[:, 1:], jnp.zeros_like(shaped[:, :1])], axis=1)
    ssm_output = results[0].reshape(replicas, sections, SEQ, WIDTH)
    param_grads = results[5].reshape(replicas, sections, 3, HEADS).sum(axis=0)
    return (ssm_output, onward(results[1]), onward(results[2]), onward(results[3]), onward(results[4]), param_grads)
```

```python
import jax
import jax.numpy as jnp
from jax import lax
from jax.experimental import pallas as pl
from jax.experimental.pallas import tpu as pltpu
from jax.sharding import Mesh
from jax.sharding import PartitionSpec as P

HEADS = 16
HEAD_DIM = 64
STATE = 128
BLOCK = 256
WIDTH = HEADS * HEAD_DIM
RANKS = 16
CTX = ("ctx_0", "ctx_1")
F32 = jnp.float32
BF16 = jnp.bfloat16
LOG2E = 1.4426950408889634
CLAMP = 64.0
INTERPRET = False


def mm(a, b, dims, precision=None):
    return lax.dot_general(
        a, b, (dims, ((), ())), precision=precision, preferred_element_type=F32
    )


def exact(a, b, dims):
    return mm(a, b, dims, lax.Precision.HIGHEST)


def triangle(lower):
    row = lax.broadcasted_iota(jnp.int32, (BLOCK, BLOCK), 0)
    col = lax.broadcasted_iota(jnp.int32, (BLOCK, BLOCK), 1)
    return row >= col if lower else row <= col


def head_of_lane():
    head = lax.broadcasted_iota(jnp.int32, (HEADS, WIDTH), 0)
    lane = lax.broadcasted_iota(jnp.int32, (HEADS, WIDTH), 1)
    return jnp.where((lane >= head * HEAD_DIM) & (lane < (head + 1) * HEAD_DIM), 1.0, 0.0)


def split(value, parts):
    pieces = []
    for _ in range(parts):
        piece = value.astype(BF16)
        pieces.append(piece)
        value = value - piece.astype(F32)
    return pieces


def expand(value, spread, parts=2):
    total = None
    for piece in split(value, parts):
        term = mm(piece, spread, ((1,), (0,)))
        total = term if total is None else total + term
    return total


def per_head(value, spread, parts=2):
    total = None
    for piece in split(value, parts):
        term = mm(piece, spread, ((1,), (1,)))
        total = term if total is None else total + term
    return total


def call(body, outs, scratch=()):
    return pl.pallas_call(
        body,
        out_shape=outs,
        scratch_shapes=scratch,
        interpret=INTERPRET,
        compiler_params=pltpu.CompilerParams(vmem_limit_bytes=48 * 1024 * 1024),
    )


def ends_kernel(
    x_ref, g_ref, b_ref, c_ref, raw_ref, log_ref, bias_ref,
    pay_ref, xs_ref, gs_ref, step_ref, run_ref,
):
    spread = head_of_lane().astype(BF16)
    raw = raw_ref[...].astype(F32) + bias_ref[...]
    step = jnp.maximum(raw, 0.0) + jnp.log1p(jnp.exp(-jnp.abs(raw)))
    rate = step * -jnp.exp(log_ref[...])
    run = exact(jnp.where(triangle(True), 1.0, 0.0), rate, ((1,), (0,)))
    last = run[BLOCK - 1 : BLOCK, :]
    step_ref[...] = step
    run_ref[...] = run
    tail = expand(jnp.exp(last - run) * step, spread)
    head = expand(jnp.exp(run), spread)
    xs = (x_ref[...].astype(F32) * tail).astype(BF16)
    gs = (g_ref[...].astype(F32) * head).astype(BF16)
    xs_ref[...] = xs
    gs_ref[...] = gs
    end = mm(xs, b_ref[...], ((0,), (0,))).astype(BF16)
    seen = mm(gs, c_ref[...], ((0,), (0,))).astype(BF16)
    drop = jnp.exp(last)
    for h in range(HEADS):
        rows = slice(h * HEAD_DIM, (h + 1) * HEAD_DIM)
        pay_ref[h, 0:64, :] = end[rows, :]
        pay_ref[h, 64:128, :] = seen[rows, :]
        high = jnp.broadcast_to(drop[:, h : h + 1], (16, STATE))
        piece = high.astype(BF16)
        pay_ref[h, 128:144, :] = piece
        pay_ref[h, 144:160, :] = (high - piece.astype(F32)).astype(BF16)


def inner_kernel(
    x_ref, g_ref, b_ref, c_ref, step_ref, run_ref,
    y_ref, dx_ref, db_ref, dc_ref, acc_ref,
):
    causal = triangle(True)
    b = b_ref[...]
    c = c_ref[...]
    scores = jnp.where(causal, mm(c, b, ((1,), (1,))), 0.0)
    running = run_ref[...] * LOG2E
    column = jnp.log(step_ref[...]) * LOG2E - running
    eye = jnp.where(causal & triangle(False), 1.0, 0.0)
    across = exact(column, eye, ((0,), (0,)))
    lane = lax.broadcasted_iota(jnp.int32, (1, 2 * HEAD_DIM), 1)
    halves = [
        jnp.where(lane < HEAD_DIM, 1.0, 0.0).astype(BF16),
        jnp.where(lane >= HEAD_DIM, 1.0, 0.0).astype(BF16),
    ]
    for pair in range(HEADS // 2):
        lanes = slice(pair * 128, (pair + 1) * 128)
        xp = x_ref[:, lanes]
        gp = g_ref[:, lanes]
        y = None
        dx = None
        for i in range(2):
            h = 2 * pair + i
            xm = xp * halves[i]
            gm = gp * halves[i]
            spread = jnp.minimum(running[:, h : h + 1] + across[h : h + 1, :], CLAMP)
            decay = jnp.exp2(spread)
            weight = (scores * decay).astype(BF16)
            y_part = mm(weight, xm, ((1,), (0,)))
            dx_part = mm(weight, gm, ((0,), (0,)))
            y = y_part if y is None else y + y_part
            dx = dx_part if dx is None else dx + dx_part
            grad = mm(gp, xm, ((1,), (1,))).astype(BF16).astype(F32) * decay
            if h == 0:
                acc_ref[...] = grad
            else:
                acc_ref[...] += grad
        y_ref[:, lanes] = y
        dx_ref[:, lanes] = dx
    grad = jnp.where(causal, acc_ref[...], 0.0).astype(BF16)
    dc_ref[...] = mm(grad, b, ((1,), (0,)))
    db_ref[...] = mm(grad, c, ((0,), (0,)))


def join_kernel(got_ref, out_ref):
    state = jnp.zeros((64, STATE), F32)
    for j in range(RANKS):
        out_ref[j, 0:64, :] = state.astype(BF16)
        drop = got_ref[j, 128:129, :].astype(F32) + got_ref[j, 144:145, :].astype(F32)
        state = state * drop + got_ref[j, 0:64, :].astype(F32)
    later = jnp.zeros((64, STATE), F32)
    for j in reversed(range(RANKS)):
        out_ref[j, 64:128, :] = later.astype(BF16)
        drop = got_ref[j, 128:129, :].astype(F32) + got_ref[j, 144:145, :].astype(F32)
        later = later * drop + got_ref[j, 64:128, :].astype(F32)


def outer_kernel(
    x_ref, g_ref, b_ref, c_ref, raw_ref, log_ref, bias_ref, gain_ref,
    xs_ref, gs_ref, step_ref, run_ref, yin_ref, dxin_ref, dbin_ref, dcin_ref, st_ref,
    y_ref, dx_ref, db_ref, dc_ref, draw_ref, par_ref,
):
    spread_f = head_of_lane()
    spread = spread_f.astype(BF16)
    x = x_ref[...].astype(F32)
    g = g_ref[...].astype(F32)
    step = step_ref[...]
    run = run_ref[...]
    last = run[BLOCK - 1 : BLOCK, :]
    gain = expand(jnp.broadcast_to(gain_ref[...], (8, HEADS)), spread, 3)[0:1, :]
    start = st_ref[:, 0:64, :].reshape(WIDTH, STATE)
    later = st_ref[:, 64:128, :].reshape(WIDTH, STATE)

    dx_out = mm(b_ref[...], later, ((1,), (1,))) * expand(jnp.exp(last - run) * step, spread)
    dx = dxin_ref[...] + dx_out
    dx_ref[...] = (dx + gain * g).astype(BF16)
    y = yin_ref[...] + mm(c_ref[...], start, ((1,), (1,))) * expand(jnp.exp(run), spread)
    y_ref[...] = (y + gain * x).astype(BF16)
    db_ref[...] = (dbin_ref[...] + mm(xs_ref[...], later, ((1,), (0,)))).astype(BF16)
    dc_ref[...] = (dcin_ref[...] + mm(gs_ref[...], start, ((1,), (0,)))).astype(BF16)

    reads = per_head(g * y, spread)
    writes = per_head(x * dx, spread)
    ones = jnp.ones((8, BLOCK), BF16)
    tails = jnp.sum(x * dx_out, axis=0, keepdims=True)
    skips = jnp.sum(g * x, axis=0, keepdims=True)
    both = start.astype(F32) * later.astype(F32)
    carried = None
    for piece in split(both, 2):
        term = mm(jnp.ones((8, STATE), BF16), piece, ((1,), (1,)))
        carried = term if carried is None else carried + term
    tails = per_head(jnp.broadcast_to(tails, (8, WIDTH)), spread, 3)[0:1, :]
    skips = per_head(jnp.broadcast_to(skips, (8, WIDTH)), spread, 3)[0:1, :]
    carried = per_head(carried, spread, 3)[0:1, :]
    ends = tails + jnp.exp(last) * carried
    slope = -jnp.exp(log_ref[...])
    d_rate = exact(jnp.where(triangle(False), 1.0, 0.0), reads - writes, ((1,), (0,))) + ends
    d_step = d_rate * slope + writes / step
    raw = raw_ref[...].astype(F32) + bias_ref[...]
    d_raw = d_step / (1.0 + jnp.exp(-raw))
    draw_ref[...] = d_raw.astype(BF16)
    par_ref[...] = jnp.zeros((8, 128), F32)
    par_ref[0:1, 0:HEADS] = jnp.sum(d_rate * step, axis=0, keepdims=True) * slope
    par_ref[1:2, 0:HEADS] = jnp.sum(d_raw, axis=0, keepdims=True)
    par_ref[2:3, 0:HEADS] = skips


def shape(dims, dtype):
    return jax.ShapeDtypeStruct(dims, dtype)


def exchange(pay):
    got = lax.all_to_all(pay, CTX, 0, 0, tiled=True)
    mine = call(join_kernel, shape((RANKS, 128, STATE), BF16))(got)
    return lax.all_to_all(mine, CTX, 0, 0, tiled=True)


def total(value):
    for axes in (CTX, ("dp",)):
        size = 1
        for name in axes:
            size *= lax.axis_size(name)
        copies = jnp.broadcast_to(value, (size, *value.shape))
        value = jnp.sum(lax.all_to_all(copies, axes, 0, 0, tiled=True), axis=0)
    return value


def relay(value):
    size = lax.axis_size("pipe")
    return lax.ppermute(value, "pipe", [(i, i - 1) for i in range(1, size)])


def on_device(x, b, c, raw, log_row, bias_row, gain_row, g):
    x, b, c, raw, g = (v[0, 0] for v in (x, b, c, raw, g))
    pay, xs, gs, step, run = call(
        ends_kernel,
        (
            shape((HEADS, 160, STATE), BF16),
            shape((BLOCK, WIDTH), BF16),
            shape((BLOCK, WIDTH), BF16),
            shape((BLOCK, HEADS), F32),
            shape((BLOCK, HEADS), F32),
        ),
    )(x, g, b, c, raw, log_row, bias_row)
    yin, dxin, dbin, dcin = call(
        inner_kernel,
        (
            shape((BLOCK, WIDTH), F32),
            shape((BLOCK, WIDTH), F32),
            shape((BLOCK, STATE), F32),
            shape((BLOCK, STATE), F32),
        ),
        (pltpu.VMEM((BLOCK, BLOCK), F32),),
    )(x, g, b, c, step, run)
    states = exchange(pay)
    y, dx, db, dc, draw, par = call(
        outer_kernel,
        (
            shape((BLOCK, WIDTH), BF16),
            shape((BLOCK, WIDTH), BF16),
            shape((BLOCK, STATE), BF16),
            shape((BLOCK, STATE), BF16),
            shape((BLOCK, HEADS), BF16),
            shape((8, 128), F32),
        ),
    )(x, g, b, c, raw, log_row, bias_row, gain_row, xs, gs, step, run, yin, dxin, dbin, dcin, states)
    dx, db, dc, draw = (relay(v) for v in (dx, db, dc, draw))
    par = total(par)[:3, :HEADS]
    return (
        y[None, None], dx[None, None], db[None, None], dc[None, None], draw[None, None], par[None],
    )


def solution(mesh):
    finer = Mesh(
        mesh.devices.reshape(mesh.shape["dp"], mesh.shape["pipe"], mesh.shape["ctx"] // 2, 2),
        ("dp", "pipe", "ctx_0", "ctx_1"),
    )
    tokens = P("dp", "pipe", CTX, None)
    row = P("pipe", None)
    return jax.shard_map(
        on_device,
        mesh=finer,
        in_specs=(tokens, tokens, tokens, tokens, row, row, row, tokens),
        out_specs=(tokens, tokens, tokens, tokens, tokens, P("pipe", None, None)),
        check_vma=False,
    )
```

```python
import jax
import jax.numpy as jnp
from jax import lax
from jax.experimental import pallas as pl
from jax.experimental.pallas import tpu as pltpu
from jax.sharding import Mesh
from jax.sharding import PartitionSpec as P

HEADS = 16
HEAD_DIM = 64
STATE = 128
BLOCK = 256
WIDTH = HEADS * HEAD_DIM
RANKS = 16
CTX = ("ctx_0", "ctx_1")
DP_CTX = ("dp", "ctx_0", "ctx_1")
F32 = jnp.float32
BF16 = jnp.bfloat16
LOG2E = 1.4426950408889634
CLAMP = 64.0
INTERPRET = False


def mm(a, b, dims, precision=None):
    return lax.dot_general(
        a, b, (dims, ((), ())), precision=precision, preferred_element_type=F32
    )


def exact(a, b, dims):
    return mm(a, b, dims, lax.Precision.HIGHEST)


def parts_mm(ones, value, dims):
    total = None
    for piece in split(value, 3):
        term = mm(ones, piece, dims)
        total = term if total is None else total + term
    return total


def triangle(lower):
    row = lax.broadcasted_iota(jnp.int32, (BLOCK, BLOCK), 0)
    col = lax.broadcasted_iota(jnp.int32, (BLOCK, BLOCK), 1)
    return row >= col if lower else row <= col


def head_of_lane():
    head = lax.broadcasted_iota(jnp.int32, (HEADS, WIDTH), 0)
    lane = lax.broadcasted_iota(jnp.int32, (HEADS, WIDTH), 1)
    return jnp.where((lane >= head * HEAD_DIM) & (lane < (head + 1) * HEAD_DIM), 1.0, 0.0)


def split(value, parts):
    pieces = []
    for _ in range(parts):
        piece = value.astype(BF16)
        pieces.append(piece)
        value = value - piece.astype(F32)
    return pieces


def expand(value, spread, parts=2):
    total = None
    for piece in split(value, parts):
        term = mm(piece, spread, ((1,), (0,)))
        total = term if total is None else total + term
    return total


def per_head(value, spread, parts=2):
    total = None
    for piece in split(value, parts):
        term = mm(piece, spread, ((1,), (1,)))
        total = term if total is None else total + term
    return total


ANY = pl.BlockSpec(memory_space=pltpu.HBM)
VMEM = pl.BlockSpec(memory_space=pltpu.VMEM)


def shape(dims, dtype):
    return jax.ShapeDtypeStruct(dims, dtype)


def chunks_of(dims):
    return 4 if dims[0] * dims[1] >= BLOCK * WIDTH else 1


def run_kernel(body, fetched, held, outs, scratch=()):
    count, near, far = len(fetched), len(held), len(outs)
    sem_count = max(count, 1)

    def kernel(*refs):
        sources = refs[:count]
        blocks = refs[count + near + far : 2 * count + near + far]
        sems = refs[2 * count + near + far]
        rest = refs[2 * count + near + far + 1 :]
        copies = []
        for k, (src, dst) in enumerate(zip(sources, blocks)):
            count_of = chunks_of(src.shape)
            rows = src.shape[0] // count_of
            copies.append(
                [
                    pltpu.make_async_copy(
                        src.at[pl.ds(i * rows, rows)], dst.at[pl.ds(i * rows, rows)], sems.at[k, i]
                    )
                    for i in range(count_of)
                ]
            )
        for group in copies:
            for copy in group:
                copy.start()

        def fetch(k):
            for copy in copies[k]:
                copy.wait()
            return blocks[k]

        body(fetch, *refs[count : count + near + far], *rest)

    return pl.pallas_call(
        kernel,
        out_shape=outs,
        in_specs=[ANY] * count + [VMEM] * near,
        out_specs=tuple([VMEM] * far),
        scratch_shapes=[pltpu.VMEM(v.shape, v.dtype) for v in fetched]
        + [pltpu.SemaphoreType.DMA((sem_count, 4))]
        + list(scratch),
        interpret=INTERPRET,
        compiler_params=pltpu.CompilerParams(vmem_limit_bytes=24 * 1024 * 1024),
    )(*(pltpu.with_memory_space_constraint(v, pltpu.HBM) for v in fetched), *held)


def identity(size):
    row = lax.broadcasted_iota(jnp.int32, (size, size), 0)
    col = lax.broadcasted_iota(jnp.int32, (size, size), 1)
    return jnp.where(row == col, 1.0, 0.0)


def upright(raw_ref):
    return mm(identity(BLOCK).astype(BF16), raw_ref[...], ((1,), (1,)))


def ends_kernel(fetch, pay_ref, time_ref):
    spread = head_of_lane().astype(BF16)
    raw = upright(fetch(0)) + fetch(2)[...]
    step = jnp.maximum(raw, 0.0) + jnp.log1p(jnp.exp(-jnp.abs(raw)))
    rate = step * -jnp.exp(fetch(1)[...])
    run = parts_mm(jnp.where(triangle(True), 1.0, 0.0).astype(BF16), rate, ((1,), (0,)))
    last = run[BLOCK - 1 : BLOCK, :]
    time_ref[0:BLOCK, :] = step
    time_ref[BLOCK : 2 * BLOCK, :] = run
    drop = jnp.exp(last)
    upper_half = lax.broadcasted_iota(jnp.int32, (8, STATE), 0) < 4
    for h in range(HEADS):
        high = jnp.broadcast_to(drop[:, h : h + 1], (8, STATE))
        piece = high.astype(BF16).astype(F32)
        pay_ref[h, 128:136, :] = jnp.where(upper_half, piece, high - piece).astype(BF16)
    head = expand(jnp.exp(run), spread)
    tail = expand(jnp.exp(last - run) * step, spread)
    gs = (fetch(3)[...].astype(F32) * head).astype(BF16)
    seen = mm(gs, fetch(4)[...], ((0,), (0,))).astype(BF16)
    for h in range(HEADS):
        pay_ref[h, 64:128, :] = seen[h * HEAD_DIM : (h + 1) * HEAD_DIM, :]
    xs = (fetch(5)[...].astype(F32) * tail).astype(BF16)
    end = mm(xs, fetch(6)[...], ((0,), (0,))).astype(BF16)
    for h in range(HEADS):
        pay_ref[h, 0:64, :] = end[h * HEAD_DIM : (h + 1) * HEAD_DIM, :]


PACK = WIDTH + 2 * STATE


def column(k):
    return slice(k * HEADS, (k + 1) * HEADS)


def inner_kernel(fetch, time_ref, out_ref, y_ref, col_ref, acc_ref):
    causal = triangle(True)
    step = time_ref[0:BLOCK, :]
    run = time_ref[BLOCK : 2 * BLOCK, :]
    last = run[BLOCK - 1 : BLOCK, :]
    running = run * LOG2E
    across = exact(jnp.log(step) * LOG2E - running, identity(BLOCK), ((0,), (0,)))
    lane = lax.broadcasted_iota(jnp.int32, (1, 2 * HEAD_DIM), 1)
    halves = [
        jnp.where(lane < HEAD_DIM, 1.0, 0.0).astype(BF16),
        jnp.where(lane >= HEAD_DIM, 1.0, 0.0).astype(BF16),
    ]
    b = fetch(2)[...]
    c = fetch(3)[...]
    scores = jnp.where(causal, mm(c, b, ((1,), (1,))), 0.0)
    x_ref = fetch(0)
    g_ref = fetch(1)
    for pair in range(HEADS // 2):
        lanes = slice(pair * 128, (pair + 1) * 128)
        xp = x_ref[:, lanes]
        gp = g_ref[:, lanes]
        y = None
        dx = None
        for i in range(2):
            h = 2 * pair + i
            xm = xp * halves[i]
            gm = gp * halves[i]
            spread = jnp.minimum(running[:, h : h + 1] + across[h : h + 1, :], CLAMP)
            decay = jnp.exp2(spread)
            weight = (scores * decay).astype(BF16)
            y_part = mm(weight, xm, ((1,), (0,)))
            dx_part = mm(weight, gm, ((0,), (0,)))
            y = y_part if y is None else y + y_part
            dx = dx_part if dx is None else dx + dx_part
            grad = mm(gp, xm, ((1,), (1,))).astype(BF16).astype(F32) * decay
            if h == 0:
                acc_ref[...] = grad
            else:
                acc_ref[...] += grad
        out_ref[:, lanes] = dx
        y_ref[:, lanes] = y
    grad = jnp.where(causal, acc_ref[...], 0.0).astype(BF16)
    out_ref[:, WIDTH : WIDTH + STATE] = mm(grad, c, ((0,), (0,)))
    out_ref[:, WIDTH + STATE : PACK] = mm(grad, b, ((1,), (0,)))
    spread = head_of_lane().astype(BF16)
    x = x_ref[...].astype(F32)
    g = g_ref[...].astype(F32)
    dx = out_ref[:, 0:WIDTH]
    y = y_ref[...]
    gain = expand(jnp.broadcast_to(fetch(7)[...], (8, HEADS)), spread, 3)[0:1, :]
    reads = per_head(g * y, spread)
    writes = per_head(x * dx, spread)
    out_ref[:, 0:WIDTH] = dx + gain * g
    y_ref[...] = y + gain * x
    skips = jnp.broadcast_to(jnp.sum(g * x, axis=0, keepdims=True), (8, WIDTH))
    skips = per_head(skips, spread, 3)[0:1, :]
    raw = upright(fetch(4)) + fetch(6)[...]
    slope = -jnp.exp(fetch(5)[...])
    col_ref[:, column(0)] = reads
    col_ref[:, column(1)] = writes
    col_ref[:, column(2)] = step
    col_ref[:, column(3)] = 1.0 / (1.0 + jnp.exp(-raw))
    col_ref[:, column(4)] = jnp.broadcast_to(slope, (BLOCK, HEADS))
    col_ref[:, column(5)] = jnp.exp(last - run) * step
    col_ref[:, column(6)] = jnp.exp(run)
    col_ref[:, column(7)] = jnp.broadcast_to(skips, (BLOCK, HEADS))


def join_kernel(fetch, got_ref, out_ref):
    def drop_of(j):
        return got_ref[j, 128:129, :].astype(F32) + got_ref[j, 132:133, :].astype(F32)

    state = jnp.zeros((64, STATE), F32)
    later = jnp.zeros((64, STATE), F32)
    for j in range(RANKS):
        k = RANKS - 1 - j
        out_ref[j, 0:64, :] = state.astype(BF16)
        out_ref[k, 64:128, :] = later.astype(BF16)
        state = state * drop_of(j) + got_ref[j, 0:64, :].astype(F32)
        later = later * drop_of(k) + got_ref[k, 64:128, :].astype(F32)


def outer_kernel(fetch, state_ref, col_ref, b_ref, c_ref, x_ref, g_ref, pack_ref, par_ref, sent_ref):
    spread = head_of_lane().astype(BF16)
    start = state_ref[:, 0:64, :].reshape(WIDTH, STATE)
    later = state_ref[:, 64:128, :].reshape(WIDTH, STATE)
    both = start.astype(F32) * later.astype(F32)
    carried = None
    for piece in split(both, 2):
        term = mm(jnp.ones((8, STATE), BF16), piece, ((1,), (1,)))
        carried = term if carried is None else carried + term
    carried = per_head(carried, spread, 3)[0:1, :]
    back = mm(b_ref[...], later, ((1,), (1,)))
    front = mm(c_ref[...], start, ((1,), (1,)))
    col = col_ref[...]
    tail = expand(col[:, column(5)], spread)
    head = expand(col[:, column(6)], spread)
    xs = x_ref[...].astype(F32) * tail
    tails = per_head(back * xs, spread)
    gs = g_ref[...].astype(F32) * head
    reads = col[:, column(0)] + per_head(front * gs, spread)
    writes = col[:, column(1)] + tails
    step = col[:, column(2)]
    slope = col[0:1, column(4)]
    drop = col[BLOCK - 1 : BLOCK, column(6)]
    ends = jnp.sum(tails, axis=0, keepdims=True) + drop * carried
    upper = jnp.where(triangle(False), 1.0, 0.0).astype(BF16)
    d_rate = parts_mm(upper, reads - writes, ((1,), (0,))) + ends
    d_raw = (d_rate * slope + writes / step) * col[:, column(3)]
    rates = jnp.sum(d_rate * step, axis=0, keepdims=True) * slope
    biases = jnp.sum(d_raw, axis=0, keepdims=True)
    flat = jnp.concatenate([rates, biases, col[0:1, column(7)]], axis=1)
    for k in range(par_ref.shape[0]):
        par_ref[k, :, 0 : 3 * HEADS] = flat
    draw = mm(d_raw.astype(BF16), identity(BLOCK).astype(BF16), ((0,), (0,)))
    sent_ref[BLOCK : BLOCK + HEADS, 0:BLOCK] = draw.astype(BF16)
    db = mm(xs.astype(BF16), later, ((1,), (0,)))
    dc = mm(gs.astype(BF16), start, ((1,), (0,)))
    sent_ref[0:BLOCK, 0:WIDTH] = (pack_ref[:, 0:WIDTH] + back * tail).astype(BF16)
    both = pack_ref[:, WIDTH:PACK] + jnp.concatenate([db, dc], axis=1)
    sent_ref[0:BLOCK, WIDTH:PACK] = both.astype(BF16)


def output_kernel(fetch, state_ref, y_ref):
    spread = head_of_lane().astype(BF16)
    start = state_ref[:, 0:64, :].reshape(WIDTH, STATE)
    front = mm(fetch(1)[...], start, ((1,), (1,)))
    head = expand(fetch(0)[...][:, column(6)], spread)
    y_ref[...] = (fetch(2)[...] + front * head).astype(BF16).reshape(y_ref.shape)


def last_kernel(got_ref, sent_ref, par_ref, dx_ref, db_ref, dc_ref, draw_ref, sems):
    copies = [
        pltpu.make_async_copy(
            sent_ref.at[pl.ds(row, rows), pl.ds(lane, lanes)], out.at[0, 0], sems.at[k]
        )
        for k, (out, row, rows, lane, lanes) in enumerate(
            (
                (dx_ref, 0, BLOCK, 0, WIDTH),
                (db_ref, 0, BLOCK, WIDTH, STATE),
                (dc_ref, 0, BLOCK, WIDTH + STATE, STATE),
                (draw_ref, BLOCK, HEADS, 0, BLOCK),
            )
        )
    ]
    for copy in copies:
        copy.start()
    flat = jnp.sum(got_ref[...], axis=0)
    for k in range(3):
        par_ref[k, :, :] = flat[:, k * HEADS : (k + 1) * HEADS]
    for copy in copies:
        copy.wait()


def spread_out(value, axes):
    return lax.all_to_all(value, axes, 0, 0, tiled=True)


def relay(value):
    size = lax.axis_size("pipe")
    return lax.ppermute(value, "pipe", [(i, i - 1) for i in range(1, size)])


def on_device(x, b, c, raw, log_row, bias_row, gain_row, g):
    x, b, c, raw, g = (v[0, 0] for v in (x, b, c, raw, g))
    raw = raw.T
    everyone = 1
    for name in DP_CTX:
        everyone *= lax.axis_size(name)
    pay, time = run_kernel(
        ends_kernel,
        (raw, log_row, bias_row, g, c, x, b),
        (),
        (shape((HEADS, 136, STATE), BF16), shape((2 * BLOCK, HEADS), F32)),
    )
    got = spread_out(pay, CTX)
    pack, base, col = run_kernel(
        inner_kernel,
        (x, g, b, c, raw, log_row, bias_row, gain_row),
        (time,),
        (shape((BLOCK, PACK), F32), shape((BLOCK, WIDTH), F32), shape((BLOCK, 8 * HEADS), F32)),
        (pltpu.VMEM((BLOCK, BLOCK), F32),),
    )
    (states,) = run_kernel(join_kernel, (), (got,), (shape((RANKS, 128, STATE), BF16),))
    states = spread_out(states, CTX)
    par, sent = run_kernel(
        outer_kernel,
        (),
        (states, col, b, c, x, g, pack),
        (shape((everyone, 1, 128), F32), shape((BLOCK + HEADS, PACK), BF16)),
    )
    sent = relay(sent)
    par = spread_out(par, DP_CTX)
    (y,) = run_kernel(
        output_kernel, (col, c, base), (states,), (shape((1, 1, BLOCK, WIDTH), BF16),)
    )
    par, dx, db, dc, draw = pl.pallas_call(
        last_kernel,
        out_shape=(
            shape((3, 1, HEADS), F32),
            shape((1, 1, BLOCK, WIDTH), BF16),
            shape((1, 1, BLOCK, STATE), BF16),
            shape((1, 1, BLOCK, STATE), BF16),
            shape((1, 1, HEADS, BLOCK), BF16),
        ),
        in_specs=[VMEM, VMEM],
        out_specs=(VMEM, ANY, ANY, ANY, ANY),
        compiler_params=pltpu.CompilerParams(vmem_limit_bytes=4 * 1024 * 1024),
        scratch_shapes=[pltpu.SemaphoreType.DMA((4,))],
        interpret=INTERPRET,
    )(par, sent)
    return y, dx, db, dc, jnp.swapaxes(draw, 2, 3), jnp.swapaxes(par, 0, 1)


def solution(mesh):
    finer = Mesh(
        mesh.devices.reshape(mesh.shape["dp"], mesh.shape["pipe"], mesh.shape["ctx"] // 2, 2),
        ("dp", "pipe", "ctx_0", "ctx_1"),
    )
    tokens = P("dp", "pipe", CTX, None)
    row = P("pipe", None)
    return jax.shard_map(
        on_device,
        mesh=finer,
        in_specs=(tokens, tokens, tokens, tokens, row, row, row, tokens),
        out_specs=(tokens, tokens, tokens, tokens, tokens, P("pipe", None, None)),
        check_vma=False,
    )
```

```python
import jax
import jax.numpy as jnp
from jax import lax
from jax.experimental import pallas as pl
from jax.experimental.pallas import tpu as pltpu
from jax.sharding import Mesh
from jax.sharding import PartitionSpec as P

HEADS = 16
HEAD_DIM = 64
STATE = 128
BLOCK = 256
WIDTH = HEADS * HEAD_DIM
RANKS = 16
CTX = ("ctx_0", "ctx_1")
DP_CTX = ("dp", "ctx_0", "ctx_1")
F32 = jnp.float32
BF16 = jnp.bfloat16
LOG2E = 1.4426950408889634
CLAMP = 64.0
INTERPRET = False


def mm(a, b, dims, precision=None):
    return lax.dot_general(
        a, b, (dims, ((), ())), precision=precision, preferred_element_type=F32
    )


def exact(a, b, dims):
    return mm(a, b, dims, lax.Precision.HIGHEST)


def parts_mm(ones, value, dims):
    total = None
    for piece in split(value, 3):
        term = mm(ones, piece, dims)
        total = term if total is None else total + term
    return total


def triangle(lower):
    row = lax.broadcasted_iota(jnp.int32, (BLOCK, BLOCK), 0)
    col = lax.broadcasted_iota(jnp.int32, (BLOCK, BLOCK), 1)
    return row >= col if lower else row <= col


def head_of_lane():
    head = lax.broadcasted_iota(jnp.int32, (HEADS, WIDTH), 0)
    lane = lax.broadcasted_iota(jnp.int32, (HEADS, WIDTH), 1)
    return jnp.where((lane >= head * HEAD_DIM) & (lane < (head + 1) * HEAD_DIM), 1.0, 0.0)


def split(value, parts):
    pieces = []
    for _ in range(parts):
        piece = value.astype(BF16)
        pieces.append(piece)
        value = value - piece.astype(F32)
    return pieces


def expand(value, spread, parts=2):
    pieces = jnp.concatenate(split(value, parts), axis=1)
    return mm(pieces, jnp.concatenate([spread] * parts, axis=0), ((1,), (0,)))


def per_head(value, spread, parts=2):
    total = None
    for piece in split(value, parts):
        term = mm(piece, spread, ((1,), (1,)))
        total = term if total is None else total + term
    return total


ANY = pl.BlockSpec(memory_space=pltpu.HBM)
VMEM = pl.BlockSpec(memory_space=pltpu.VMEM)


def shape(dims, dtype):
    return jax.ShapeDtypeStruct(dims, dtype)


def chunks_of(dims):
    return 4 if dims[0] * dims[1] >= BLOCK * WIDTH else 1


def run_kernel(body, fetched, held, outs, scratch=()):
    count, near, far = len(fetched), len(held), len(outs)
    sem_count = max(count, 1)

    def kernel(*refs):
        sources = refs[:count]
        blocks = refs[count + near + far : 2 * count + near + far]
        sems = refs[2 * count + near + far]
        rest = refs[2 * count + near + far + 1 :]
        copies = []
        for k, (src, dst) in enumerate(zip(sources, blocks)):
            count_of = chunks_of(src.shape)
            rows = src.shape[0] // count_of
            copies.append(
                [
                    pltpu.make_async_copy(
                        src.at[pl.ds(i * rows, rows)], dst.at[pl.ds(i * rows, rows)], sems.at[k, i]
                    )
                    for i in range(count_of)
                ]
            )
        for group in copies:
            for copy in group:
                copy.start()

        def fetch(k):
            for copy in copies[k]:
                copy.wait()
            return blocks[k]

        body(fetch, *refs[count : count + near + far], *rest)

    return pl.pallas_call(
        kernel,
        out_shape=outs,
        in_specs=[ANY] * count + [VMEM] * near,
        out_specs=tuple([VMEM] * far),
        scratch_shapes=[pltpu.VMEM(v.shape, v.dtype) for v in fetched]
        + [pltpu.SemaphoreType.DMA((sem_count, 4))]
        + list(scratch),
        interpret=INTERPRET,
        compiler_params=pltpu.CompilerParams(vmem_limit_bytes=24 * 1024 * 1024),
    )(*(pltpu.with_memory_space_constraint(v, pltpu.HBM) for v in fetched), *held)


def identity(size):
    row = lax.broadcasted_iota(jnp.int32, (size, size), 0)
    col = lax.broadcasted_iota(jnp.int32, (size, size), 1)
    return jnp.where(row == col, 1.0, 0.0)


def upright(raw_ref):
    return mm(identity(BLOCK).astype(BF16), raw_ref[...], ((1,), (1,)))


def ends_kernel(fetch, pay_ref, time_ref):
    spread = head_of_lane().astype(BF16)
    raw = upright(fetch(0)) + fetch(2)[...]
    step = jnp.maximum(raw, 0.0) + jnp.log1p(jnp.exp(-jnp.abs(raw)))
    rate = step * -jnp.exp(fetch(1)[...])
    run = parts_mm(jnp.where(triangle(True), 1.0, 0.0).astype(BF16), rate, ((1,), (0,)))
    last = run[BLOCK - 1 : BLOCK, :]
    time_ref[0:BLOCK, :] = step
    time_ref[BLOCK : 2 * BLOCK, :] = run
    drop = jnp.exp(last)
    upper_half = lax.broadcasted_iota(jnp.int32, (8, STATE), 0) < 4
    for h in range(HEADS):
        high = jnp.broadcast_to(drop[:, h : h + 1], (8, STATE))
        piece = high.astype(BF16).astype(F32)
        pay_ref[h, 128:136, :] = jnp.where(upper_half, piece, high - piece).astype(BF16)
    head = expand(jnp.exp(run), spread)
    tail = expand(jnp.exp(last - run) * step, spread)
    gs = (fetch(3)[...].astype(F32) * head).astype(BF16)
    seen = mm(fetch(4)[...], gs, ((0,), (0,))).T.astype(BF16)
    for h in range(HEADS):
        pay_ref[h, 64:128, :] = seen[h * HEAD_DIM : (h + 1) * HEAD_DIM, :]
    xs = (fetch(5)[...].astype(F32) * tail).astype(BF16)
    end = mm(fetch(6)[...], xs, ((0,), (0,))).T.astype(BF16)
    for h in range(HEADS):
        pay_ref[h, 0:64, :] = end[h * HEAD_DIM : (h + 1) * HEAD_DIM, :]


PACK = WIDTH + 2 * STATE
SENT = WIDTH // HEAD_DIM + 9


def column(k):
    return slice(2 * STATE + k * HEADS, 2 * STATE + (k + 1) * HEADS)


def inner_kernel(
    fetch, time_ref, lead_ref, pack_ref, out_ref, y_ref, blank_ref, dx_ref, acc_ref
):
    blank_ref[...] = jnp.zeros(blank_ref.shape, F32)
    causal = triangle(True)
    step = time_ref[0:BLOCK, :]
    run = time_ref[BLOCK : 2 * BLOCK, :]
    last = run[BLOCK - 1 : BLOCK, :]
    running = run * LOG2E
    across = exact(jnp.log(step) * LOG2E - running, identity(BLOCK), ((0,), (0,)))
    lane = lax.broadcasted_iota(jnp.int32, (1, 2 * HEAD_DIM), 1)
    halves = [
        jnp.where(lane < HEAD_DIM, 1.0, 0.0).astype(BF16),
        jnp.where(lane >= HEAD_DIM, 1.0, 0.0).astype(BF16),
    ]
    b = fetch(2)[...]
    c = fetch(3)[...]
    scores = jnp.where(causal, mm(c, b, ((1,), (1,))), 0.0)
    x_ref = fetch(0)
    g_ref = fetch(1)
    for pair in range(HEADS // 2):
        lanes = slice(pair * 128, (pair + 1) * 128)
        xp = x_ref[:, lanes]
        gp = g_ref[:, lanes]
        y = None
        dx = None
        for i in range(2):
            h = 2 * pair + i
            xm = xp * halves[i]
            gm = gp * halves[i]
            spread = jnp.minimum(running[:, h : h + 1] + across[h : h + 1, :], CLAMP)
            decay = jnp.exp2(spread)
            weight = (scores * decay).astype(BF16)
            y_part = mm(weight, xm, ((1,), (0,)))
            dx_part = mm(weight, gm, ((0,), (0,)))
            y = y_part if y is None else y + y_part
            dx = dx_part if dx is None else dx + dx_part
            grad = mm(gp, xm, ((1,), (1,))).astype(BF16).astype(F32) * decay
            if h == 0:
                acc_ref[...] = grad
            else:
                acc_ref[...] += grad
        dx_ref[:, lanes] = dx
        y_ref[:, lanes] = y
    grad = jnp.where(causal, acc_ref[...], 0.0).astype(BF16)
    out_ref[:, 0:STATE] = mm(grad, c, ((0,), (0,)))
    out_ref[:, STATE : 2 * STATE] = mm(grad, b, ((1,), (0,)))
    spread = head_of_lane().astype(BF16)
    x = x_ref[...].astype(F32)
    g = g_ref[...].astype(F32)
    dx = dx_ref[...]
    y = y_ref[...]
    gain = expand(jnp.broadcast_to(fetch(7)[...], (8, HEADS)), spread, 3)[0:1, :]
    reads = per_head(g * y, spread)
    writes = per_head(x * dx, spread)
    y_ref[...] = y + gain * x
    head = jnp.exp(run)
    tail = jnp.exp(last - run) * step
    high, low = split(tail, 2)
    lead_ref[:, 0:WIDTH] = (dx + gain * g).astype(BF16)
    lead_ref[:, WIDTH : WIDTH + STATE] = b
    lead_ref[:, WIDTH + STATE : WIDTH + STATE + 2 * HEADS] = jnp.concatenate([high, low], axis=1)
    pack_ref[:, 0:WIDTH] = (x * expand(tail, spread)).astype(BF16)
    pack_ref[:, WIDTH : 2 * WIDTH] = (g * expand(head, spread)).astype(BF16)
    pack_ref[:, 2 * WIDTH : 2 * WIDTH + STATE] = b
    pack_ref[:, 2 * WIDTH + STATE : 2 * WIDTH + 2 * STATE] = c
    skips = jnp.broadcast_to(jnp.sum(g * x, axis=0, keepdims=True), (8, WIDTH))
    skips = per_head(skips, spread, 3)[0:1, :]
    raw = upright(fetch(4)) + fetch(6)[...]
    slope = -jnp.exp(fetch(5)[...])
    out_ref[:, column(0)] = reads
    out_ref[:, column(1)] = writes
    out_ref[:, column(2)] = step
    out_ref[:, column(3)] = 1.0 / (1.0 + jnp.exp(-raw))
    out_ref[:, column(4)] = jnp.broadcast_to(slope, (BLOCK, HEADS))
    out_ref[:, column(5)] = jnp.broadcast_to(jnp.exp(last), (BLOCK, HEADS))
    out_ref[:, column(6)] = head
    out_ref[:, column(7)] = jnp.broadcast_to(skips, (BLOCK, HEADS))


def join_kernel(fetch, got_ref, acc_ref, out_ref):
    def drop_of(j):
        return got_ref[j, 128:129, :].astype(F32) + got_ref[j, 132:133, :].astype(F32)

    state = jnp.zeros((64, STATE), F32)
    later = jnp.zeros((64, STATE), F32)
    for j in range(RANKS):
        k = RANKS - 1 - j
        out_ref[j, 0:64, :] = state.astype(BF16)
        out_ref[k, 64:128, :] = later.astype(BF16)
        state = state * drop_of(j) + got_ref[j, 0:64, :].astype(F32)
        later = later * drop_of(k) + got_ref[k, 64:128, :].astype(F32)


def outer_kernel(blank_ref, state_ref, pack_ref, acc_ref, par_out, sent_out, par_ref, sent_ref, sems):
    copies = [
        pltpu.make_async_copy(state_ref.at[:, 64:128, :], sent_out.at[0:HEADS], sems.at[0]),
        pltpu.make_async_copy(par_ref, par_out, sems.at[1]),
        pltpu.make_async_copy(sent_ref, sent_out.at[HEADS:SENT], sems.at[2]),
    ]
    copies[0].start()
    spread = head_of_lane().astype(BF16)
    start = state_ref[:, 0:64, :].reshape(WIDTH, STATE)
    later = state_ref[:, 64:128, :].reshape(WIDTH, STATE)
    both = (start.astype(F32) * later.astype(F32)).astype(BF16)
    carried = mm(jnp.ones((8, STATE), BF16), both, ((1,), (1,)))
    carried = per_head(carried, spread)[0:1, :]
    xs = pack_ref[:, 0:WIDTH]
    gs = pack_ref[:, WIDTH : 2 * WIDTH]
    back = mm(pack_ref[:, 2 * WIDTH : 2 * WIDTH + STATE], later, ((1,), (1,)))
    tails = per_head(back * xs.astype(F32), spread, 1)
    front = mm(pack_ref[:, 2 * WIDTH + STATE : 2 * WIDTH + 2 * STATE], start, ((1,), (1,)))
    reads = acc_ref[:, column(0)] + per_head(front * gs.astype(F32), spread, 1)
    writes = acc_ref[:, column(1)] + tails
    step = acc_ref[:, column(2)]
    slope = acc_ref[0:1, column(4)]
    ends = jnp.sum(tails, axis=0, keepdims=True) + acc_ref[0:1, column(5)] * carried
    upper = jnp.where(triangle(False), 1.0, 0.0).astype(BF16)
    d_rate = parts_mm(upper, reads - writes, ((1,), (0,))) + ends
    d_raw = (d_rate * slope + writes / step) * acc_ref[:, column(3)]
    rates = jnp.sum(d_rate * step, axis=0, keepdims=True) * slope
    biases = jnp.sum(d_raw, axis=0, keepdims=True)
    flat = jnp.concatenate([rates, biases, acc_ref[0:1, column(7)]], axis=1)
    for k in range(par_ref.shape[0]):
        par_ref[k, :, 0 : 3 * HEADS] = flat
    copies[1].start()
    draw = mm(d_raw.astype(BF16), identity(BLOCK).astype(BF16), ((0,), (0,))).astype(BF16)
    sent_ref[8, 0:HEADS, :] = draw[:, 0:128]
    sent_ref[8, HEADS : 2 * HEADS, :] = draw[:, 128:256]
    db = acc_ref[:, 0:STATE] + mm(xs, later, ((1,), (0,)))
    sent_ref[0:4, :, :] = db.astype(BF16).reshape(4, HEAD_DIM, STATE)
    dc = acc_ref[:, STATE : 2 * STATE] + mm(gs, start, ((1,), (0,)))
    sent_ref[4:8, :, :] = dc.astype(BF16).reshape(4, HEAD_DIM, STATE)
    copies[2].start()
    for copy in copies:
        copy.wait()


def output_kernel(fetch, state_ref, pack_ref, acc_ref, base_ref, y_ref):
    spread = head_of_lane().astype(BF16)
    start = state_ref[:, 0:64, :].reshape(WIDTH, STATE)
    front = mm(pack_ref[:, 2 * WIDTH + STATE : 2 * WIDTH + 2 * STATE], start, ((1,), (1,)))
    head = expand(acc_ref[:, column(6)], spread)
    y_ref[...] = (base_ref[...] + front * head).astype(BF16).reshape(y_ref.shape)


def received_kernel(
    lead_ref, sent_ref, dx_out, db_out, dc_out, draw_out, dx_ref, sems
):
    copies = [
        pltpu.make_async_copy(
            sent_ref.at[HEADS + 4 * k + i],
            out.at[0, 0, pl.ds(i * HEAD_DIM, HEAD_DIM)],
            sems.at[4 * k + i],
        )
        for k, out in enumerate((db_out, dc_out))
        for i in range(4)
    ]
    copies += [
        pltpu.make_async_copy(
            sent_ref.at[HEADS + 8, pl.ds(i * HEADS, HEADS)],
            draw_out.at[0, 0, :, pl.ds(i * 128, 128)],
            sems.at[8 + i],
        )
        for i in range(2)
    ]
    for copy in copies:
        copy.start()
    spread = head_of_lane().astype(BF16)
    spread = jnp.concatenate([spread, spread], axis=0)
    at = WIDTH + STATE
    b = lead_ref[:, WIDTH:at]
    factors = lead_ref[:, at : at + 2 * HEADS]
    for k in range(4):
        lanes = slice(k * 256, (k + 1) * 256)
        later = sent_ref[4 * k : 4 * k + 4, :, :].reshape(256, STATE)
        back = mm(b, later, ((1,), (1,))) * mm(factors, spread[:, lanes], ((1,), (0,)))
        dx_ref[:, lanes] = (lead_ref[:, lanes].astype(F32) + back).astype(BF16)
        copy = pltpu.make_async_copy(
            dx_ref.at[:, pl.ds(k * 256, 256)],
            dx_out.at[0, 0, :, pl.ds(k * 256, 256)],
            sems.at[10 + k],
        )
        copy.start()
        copies.append(copy)
    for copy in copies:
        copy.wait()


def fold_kernel(fetch, got_ref, out_ref):
    flat = jnp.sum(got_ref[...], axis=0)
    for k in range(3):
        out_ref[k, :, :] = flat[:, k * HEADS : (k + 1) * HEADS]


def spread_out(value, axes):
    return lax.all_to_all(value, axes, 0, 0, tiled=True)


def relay(value):
    size = lax.axis_size("pipe")
    return lax.ppermute(value, "pipe", [(i, i - 1) for i in range(1, size)])


def layer(x, b, c, raw, log_row, bias_row, gain_row, g):
    x, b, c, raw, g = (v[0, 0] for v in (x, b, c, raw, g))
    raw = raw.T
    everyone = 1
    for name in DP_CTX:
        everyone *= lax.axis_size(name)
    pay, time = run_kernel(
        ends_kernel,
        (raw, log_row, bias_row, g, c, x, b),
        (),
        (shape((HEADS, 136, STATE), BF16), shape((2 * BLOCK, HEADS), F32)),
    )
    got = spread_out(pay, CTX)
    lead, pack, acc, base, blank = run_kernel(
        inner_kernel,
        (x, g, b, c, raw, log_row, bias_row, gain_row),
        (time,),
        (
            shape((BLOCK, PACK), BF16),
            shape((BLOCK, 2 * WIDTH + 2 * STATE), BF16),
            shape((BLOCK, 2 * STATE + 8 * HEADS), F32),
            shape((BLOCK, WIDTH), F32),
            shape((everyone, 1, 128), F32),
        ),
        (pltpu.VMEM((BLOCK, WIDTH), F32), pltpu.VMEM((BLOCK, BLOCK), F32)),
    )
    lead = relay(lead)
    (states,) = run_kernel(join_kernel, (), (got, acc), (shape((RANKS, 128, STATE), BF16),))
    states = spread_out(states, CTX)
    blank = pltpu.with_memory_space_constraint(blank, pltpu.HBM)
    par, sent = pl.pallas_call(
        outer_kernel,
        out_shape=(shape((everyone, 1, 128), F32), shape((SENT, HEAD_DIM, STATE), BF16)),
        in_specs=[ANY] + [VMEM] * 3,
        out_specs=(ANY, ANY),
        input_output_aliases={0: 0},
        scratch_shapes=[
            pltpu.VMEM((everyone, 1, 128), F32),
            pltpu.VMEM((9, HEAD_DIM, STATE), BF16),
            pltpu.SemaphoreType.DMA((3,)),
        ],
        interpret=INTERPRET,
        compiler_params=pltpu.CompilerParams(vmem_limit_bytes=24 * 1024 * 1024),
    )(blank, states, pack, acc)
    sent = relay(sent)
    par = spread_out(par, DP_CTX)
    (y,) = run_kernel(
        output_kernel, (), (states, pack, acc, base), (shape((1, 1, BLOCK, WIDTH), BF16),)
    )
    dx, db, dc, draw = pl.pallas_call(
        received_kernel,
        out_shape=(
            shape((1, 1, BLOCK, WIDTH), BF16),
            shape((1, 1, BLOCK, STATE), BF16),
            shape((1, 1, BLOCK, STATE), BF16),
            shape((1, 1, HEADS, BLOCK), BF16),
        ),
        in_specs=[VMEM] * 2,
        out_specs=(ANY, ANY, ANY, ANY),
        scratch_shapes=[pltpu.VMEM((BLOCK, WIDTH), BF16), pltpu.SemaphoreType.DMA((14,))],
        interpret=INTERPRET,
        compiler_params=pltpu.CompilerParams(vmem_limit_bytes=12 * 1024 * 1024),
    )(lead, sent)
    (par,) = run_kernel(fold_kernel, (), (par,), (shape((3, 1, HEADS), F32),))
    return y, dx, db, dc, jnp.swapaxes(draw, 2, 3), jnp.swapaxes(par, 0, 1)


def solution(mesh):
    finer = Mesh(
        mesh.devices.reshape(mesh.shape["dp"], mesh.shape["pipe"], mesh.shape["ctx"] // 2, 2),
        ("dp", "pipe", "ctx_0", "ctx_1"),
    )
    tokens = P("dp", "pipe", CTX, None)
    row = P("pipe", None)
    return jax.shard_map(
        layer,
        mesh=finer,
        in_specs=(tokens, tokens, tokens, tokens, row, row, row, tokens),
        out_specs=(tokens, tokens, tokens, tokens, tokens, P("pipe", None, None)),
        check_vma=False,
    )
```

```python
import jax
import jax.numpy as jnp
from jax import lax
from jax.experimental import pallas as pl
from jax.experimental.pallas import tpu as pltpu
from jax.sharding import Mesh
from jax.sharding import PartitionSpec as P

HEADS = 16
HEAD_DIM = 64
STATE = 128
BLOCK = 256
WIDTH = HEADS * HEAD_DIM
RANKS = 16
CTX = ("ctx_0", "ctx_1")
DP_CTX = ("dp", "ctx_0", "ctx_1")
F32 = jnp.float32
BF16 = jnp.bfloat16
LOG2E = 1.4426950408889634
CLAMP = 64.0
INTERPRET = False


def mm(a, b, dims, precision=None):
    return lax.dot_general(
        a, b, (dims, ((), ())), precision=precision, preferred_element_type=F32
    )


def exact(a, b, dims):
    return mm(a, b, dims, lax.Precision.HIGHEST)


def parts_mm(ones, value, dims):
    total = None
    for piece in split(value, 3):
        term = mm(ones, piece, dims)
        total = term if total is None else total + term
    return total


def triangle(lower):
    row = lax.broadcasted_iota(jnp.int32, (BLOCK, BLOCK), 0)
    col = lax.broadcasted_iota(jnp.int32, (BLOCK, BLOCK), 1)
    return row >= col if lower else row <= col


def head_of_lane():
    head = lax.broadcasted_iota(jnp.int32, (HEADS, WIDTH), 0)
    lane = lax.broadcasted_iota(jnp.int32, (HEADS, WIDTH), 1)
    return jnp.where((lane >= head * HEAD_DIM) & (lane < (head + 1) * HEAD_DIM), 1.0, 0.0)


def split(value, parts):
    pieces = []
    for _ in range(parts):
        piece = value.astype(BF16)
        pieces.append(piece)
        value = value - piece.astype(F32)
    return pieces


def expand(value, spread, parts=2):
    pieces = jnp.concatenate(split(value, parts), axis=1)
    return mm(pieces, jnp.concatenate([spread] * parts, axis=0), ((1,), (0,)))


def per_head(value, spread, parts=2):
    total = None
    for piece in split(value, parts):
        term = mm(piece, spread, ((1,), (1,)))
        total = term if total is None else total + term
    return total


ANY = pl.BlockSpec(memory_space=pltpu.HBM)
VMEM = pl.BlockSpec(memory_space=pltpu.VMEM)


def shape(dims, dtype):
    return jax.ShapeDtypeStruct(dims, dtype)


def chunks_of(dims):
    return 4 if dims[0] * dims[1] >= BLOCK * WIDTH else 1


def run_kernel(body, fetched, held, outs, scratch=(), grant=24, far_outs=0):
    count, near, far = len(fetched), len(held), len(outs)
    sem_count = max(count, 1)

    def kernel(*refs):
        sources = refs[:count]
        blocks = refs[count + near + far : 2 * count + near + far]
        sems = refs[2 * count + near + far]
        rest = refs[2 * count + near + far + 1 :]
        copies = []
        for k, (src, dst) in enumerate(zip(sources, blocks)):
            count_of = chunks_of(src.shape)
            rows = src.shape[0] // count_of
            copies.append(
                [
                    pltpu.make_async_copy(
                        src.at[pl.ds(i * rows, rows)], dst.at[pl.ds(i * rows, rows)], sems.at[k, i]
                    )
                    for i in range(count_of)
                ]
            )
        for group in copies:
            for copy in group:
                copy.start()

        def fetch(k):
            for copy in copies[k]:
                copy.wait()
            return blocks[k]

        body(fetch, *refs[count : count + near + far], *rest)

    return pl.pallas_call(
        kernel,
        out_shape=outs,
        in_specs=[ANY] * count + [VMEM] * near,
        out_specs=tuple([ANY] * far_outs + [VMEM] * (far - far_outs)),
        scratch_shapes=[pltpu.VMEM(v.shape, v.dtype) for v in fetched]
        + [pltpu.SemaphoreType.DMA((sem_count, 4))]
        + list(scratch),
        interpret=INTERPRET,
        compiler_params=pltpu.CompilerParams(vmem_limit_bytes=grant * 1024 * 1024),
    )(*(pltpu.with_memory_space_constraint(v, pltpu.HBM) for v in fetched), *held)


def identity(size):
    row = lax.broadcasted_iota(jnp.int32, (size, size), 0)
    col = lax.broadcasted_iota(jnp.int32, (size, size), 1)
    return jnp.where(row == col, 1.0, 0.0)


def upright(raw_ref):
    return mm(identity(BLOCK).astype(BF16), raw_ref[...], ((1,), (1,)))


def ends_kernel(fetch, pay_out, time_ref, pay_ref, out_sems):
    halves = (slice(64, 136), slice(0, 64))
    copies = [
        pltpu.make_async_copy(pay_ref.at[:, rows, :], pay_out.at[:, rows, :], out_sems.at[k])
        for k, rows in enumerate(halves)
    ]
    spread = head_of_lane().astype(BF16)
    raw = upright(fetch(0)) + fetch(2)[...]
    step = jnp.maximum(raw, 0.0) + jnp.log1p(jnp.exp(-jnp.abs(raw)))
    rate = step * -jnp.exp(fetch(1)[...])
    run = parts_mm(jnp.where(triangle(True), 1.0, 0.0).astype(BF16), rate, ((1,), (0,)))
    last = run[BLOCK - 1 : BLOCK, :]
    time_ref[0:BLOCK, :] = step
    time_ref[BLOCK : 2 * BLOCK, :] = run
    drop = jnp.exp(last)
    upper_half = lax.broadcasted_iota(jnp.int32, (8, STATE), 0) < 4
    for h in range(HEADS):
        high = jnp.broadcast_to(drop[:, h : h + 1], (8, STATE))
        piece = high.astype(BF16).astype(F32)
        pay_ref[h, 128:136, :] = jnp.where(upper_half, piece, high - piece).astype(BF16)
    head = expand(jnp.exp(run), spread)
    gs = (fetch(3)[...].astype(F32) * head).astype(BF16)
    seen = mm(fetch(4)[...], gs, ((0,), (0,))).T.astype(BF16)
    for h in range(HEADS):
        pay_ref[h, 64:128, :] = seen[h * HEAD_DIM : (h + 1) * HEAD_DIM, :]
    copies[0].start()
    tail = expand(jnp.exp(last - run) * step, spread)
    xs = (fetch(5)[...].astype(F32) * tail).astype(BF16)
    end = mm(fetch(6)[...], xs, ((0,), (0,))).T.astype(BF16)
    for h in range(HEADS):
        pay_ref[h, 0:64, :] = end[h * HEAD_DIM : (h + 1) * HEAD_DIM, :]
    copies[1].start()
    for copy in copies:
        copy.wait()


PACK = WIDTH + 2 * STATE
SENT = WIDTH // HEAD_DIM + 9


def column(k):
    return slice(2 * STATE + k * HEADS, 2 * STATE + (k + 1) * HEADS)


def inner_kernel(
    fetch, time_ref, lead_ref, pack_ref, out_ref, y_ref, blank_ref, dx_ref, acc_ref
):
    blank_ref[...] = jnp.zeros(blank_ref.shape, F32)
    causal = triangle(True)
    step = time_ref[0:BLOCK, :]
    run = time_ref[BLOCK : 2 * BLOCK, :]
    last = run[BLOCK - 1 : BLOCK, :]
    running = run * LOG2E
    across = exact(jnp.log(step) * LOG2E - running, identity(BLOCK), ((0,), (0,)))
    lane = lax.broadcasted_iota(jnp.int32, (1, 2 * HEAD_DIM), 1)
    halves = [
        jnp.where(lane < HEAD_DIM, 1.0, 0.0).astype(BF16),
        jnp.where(lane >= HEAD_DIM, 1.0, 0.0).astype(BF16),
    ]
    b = fetch(2)[...]
    c = fetch(3)[...]
    scores = jnp.where(causal, mm(c, b, ((1,), (1,))), 0.0)
    x_ref = fetch(0)
    g_ref = fetch(1)
    for pair in range(HEADS // 2):
        lanes = slice(pair * 128, (pair + 1) * 128)
        xp = x_ref[:, lanes]
        gp = g_ref[:, lanes]
        y = None
        dx = None
        for i in range(2):
            h = 2 * pair + i
            xm = xp * halves[i]
            gm = gp * halves[i]
            spread = jnp.minimum(running[:, h : h + 1] + across[h : h + 1, :], CLAMP)
            decay = jnp.exp2(spread)
            weight = (scores * decay).astype(BF16)
            y_part = mm(weight, xm, ((1,), (0,)))
            dx_part = mm(weight, gm, ((0,), (0,)))
            y = y_part if y is None else y + y_part
            dx = dx_part if dx is None else dx + dx_part
            grad = mm(gp, xm, ((1,), (1,))).astype(BF16).astype(F32) * decay
            if h == 0:
                acc_ref[...] = grad
            else:
                acc_ref[...] += grad
        dx_ref[:, lanes] = dx
        y_ref[:, lanes] = y
    grad = jnp.where(causal, acc_ref[...], 0.0).astype(BF16)
    out_ref[:, 0:STATE] = mm(grad, c, ((0,), (0,)))
    out_ref[:, STATE : 2 * STATE] = mm(grad, b, ((1,), (0,)))
    spread = head_of_lane().astype(BF16)
    x = x_ref[...].astype(F32)
    g = g_ref[...].astype(F32)
    dx = dx_ref[...]
    y = y_ref[...]
    gain = expand(jnp.broadcast_to(fetch(7)[...], (8, HEADS)), spread, 3)[0:1, :]
    reads = per_head(g * y, spread)
    writes = per_head(x * dx, spread)
    y_ref[...] = y + gain * x
    head = jnp.exp(run)
    tail = jnp.exp(last - run) * step
    high, low = split(tail, 2)
    lead_ref[:, 0:WIDTH] = (dx + gain * g).astype(BF16)
    lead_ref[:, WIDTH : WIDTH + STATE] = b
    lead_ref[:, WIDTH + STATE : WIDTH + STATE + 2 * HEADS] = jnp.concatenate([high, low], axis=1)
    pack_ref[:, 0:WIDTH] = (x * expand(tail, spread)).astype(BF16)
    pack_ref[:, WIDTH : 2 * WIDTH] = (g * expand(head, spread)).astype(BF16)
    pack_ref[:, 2 * WIDTH : 2 * WIDTH + STATE] = b
    pack_ref[:, 2 * WIDTH + STATE : 2 * WIDTH + 2 * STATE] = c
    skips = jnp.broadcast_to(jnp.sum(g * x, axis=0, keepdims=True), (8, WIDTH))
    skips = per_head(skips, spread, 3)[0:1, :]
    raw = upright(fetch(4)) + fetch(6)[...]
    slope = -jnp.exp(fetch(5)[...])
    out_ref[:, column(0)] = reads
    out_ref[:, column(1)] = writes
    out_ref[:, column(2)] = step
    out_ref[:, column(3)] = 1.0 / (1.0 + jnp.exp(-raw))
    out_ref[:, column(4)] = jnp.broadcast_to(slope, (BLOCK, HEADS))
    out_ref[:, column(5)] = jnp.broadcast_to(jnp.exp(last), (BLOCK, HEADS))
    out_ref[:, column(6)] = head
    out_ref[:, column(7)] = jnp.broadcast_to(skips, (BLOCK, HEADS))


def join_kernel(fetch, got_ref, acc_ref, out_ref):
    def drop_of(j):
        return got_ref[j, 128:129, :].astype(F32) + got_ref[j, 132:133, :].astype(F32)

    state = jnp.zeros((64, STATE), F32)
    later = jnp.zeros((64, STATE), F32)
    for j in range(RANKS):
        k = RANKS - 1 - j
        out_ref[j, 0:64, :] = state.astype(BF16)
        out_ref[k, 64:128, :] = later.astype(BF16)
        state = state * drop_of(j) + got_ref[j, 0:64, :].astype(F32)
        later = later * drop_of(k) + got_ref[k, 64:128, :].astype(F32)


def outer_kernel(blank_ref, state_ref, pack_ref, acc_ref, par_out, sent_out, par_ref, sent_ref, sems):
    copies = [
        pltpu.make_async_copy(state_ref.at[:, 64:128, :], sent_out.at[0:HEADS], sems.at[0]),
        pltpu.make_async_copy(par_ref, par_out, sems.at[1]),
        pltpu.make_async_copy(sent_ref, sent_out.at[HEADS:SENT], sems.at[2]),
    ]
    copies[0].start()
    spread = head_of_lane().astype(BF16)
    start = state_ref[:, 0:64, :].reshape(WIDTH, STATE)
    later = state_ref[:, 64:128, :].reshape(WIDTH, STATE)
    both = (start.astype(F32) * later.astype(F32)).astype(BF16)
    carried = mm(jnp.ones((8, STATE), BF16), both, ((1,), (1,)))
    carried = per_head(carried, spread)[0:1, :]
    xs = pack_ref[:, 0:WIDTH]
    gs = pack_ref[:, WIDTH : 2 * WIDTH]
    back = mm(pack_ref[:, 2 * WIDTH : 2 * WIDTH + STATE], later, ((1,), (1,)))
    tails = per_head(back * xs.astype(F32), spread, 1)
    front = mm(pack_ref[:, 2 * WIDTH + STATE : 2 * WIDTH + 2 * STATE], start, ((1,), (1,)))
    reads = acc_ref[:, column(0)] + per_head(front * gs.astype(F32), spread, 1)
    writes = acc_ref[:, column(1)] + tails
    step = acc_ref[:, column(2)]
    slope = acc_ref[0:1, column(4)]
    ends = jnp.sum(tails, axis=0, keepdims=True) + acc_ref[0:1, column(5)] * carried
    upper = jnp.where(triangle(False), 1.0, 0.0).astype(BF16)
    d_rate = parts_mm(upper, reads - writes, ((1,), (0,))) + ends
    d_raw = (d_rate * slope + writes / step) * acc_ref[:, column(3)]
    rates = jnp.sum(d_rate * step, axis=0, keepdims=True) * slope
    biases = jnp.sum(d_raw, axis=0, keepdims=True)
    flat = jnp.concatenate([rates, biases, acc_ref[0:1, column(7)]], axis=1)
    for k in range(par_ref.shape[0]):
        par_ref[k, :, 0 : 3 * HEADS] = flat
    copies[1].start()
    draw = mm(d_raw.astype(BF16), identity(BLOCK).astype(BF16), ((0,), (0,))).astype(BF16)
    sent_ref[8, 0:HEADS, :] = draw[:, 0:128]
    sent_ref[8, HEADS : 2 * HEADS, :] = draw[:, 128:256]
    db = acc_ref[:, 0:STATE] + mm(xs, later, ((1,), (0,)))
    sent_ref[0:4, :, :] = db.astype(BF16).reshape(4, HEAD_DIM, STATE)
    dc = acc_ref[:, STATE : 2 * STATE] + mm(gs, start, ((1,), (0,)))
    sent_ref[4:8, :, :] = dc.astype(BF16).reshape(4, HEAD_DIM, STATE)
    copies[2].start()
    for copy in copies:
        copy.wait()


def output_kernel(fetch, state_ref, pack_ref, acc_ref, base_ref, y_ref):
    spread = head_of_lane().astype(BF16)
    start = state_ref[:, 0:64, :].reshape(WIDTH, STATE)
    front = mm(pack_ref[:, 2 * WIDTH + STATE : 2 * WIDTH + 2 * STATE], start, ((1,), (1,)))
    head = expand(acc_ref[:, column(6)], spread)
    y_ref[...] = (base_ref[...] + front * head).astype(BF16).reshape(y_ref.shape)


def received_kernel(
    lead_ref, sent_ref, dx_out, db_out, dc_out, draw_out, dx_ref, sems
):
    copies = [
        pltpu.make_async_copy(
            sent_ref.at[HEADS + 4 * k + i],
            out.at[0, 0, pl.ds(i * HEAD_DIM, HEAD_DIM)],
            sems.at[4 * k + i],
        )
        for k, out in enumerate((db_out, dc_out))
        for i in range(4)
    ]
    copies += [
        pltpu.make_async_copy(
            sent_ref.at[HEADS + 8, pl.ds(i * HEADS, HEADS)],
            draw_out.at[0, 0, :, pl.ds(i * 128, 128)],
            sems.at[8 + i],
        )
        for i in range(2)
    ]
    for copy in copies:
        copy.start()
    spread = head_of_lane().astype(BF16)
    spread = jnp.concatenate([spread, spread], axis=0)
    at = WIDTH + STATE
    b = lead_ref[:, WIDTH:at]
    factors = lead_ref[:, at : at + 2 * HEADS]
    for k in range(4):
        lanes = slice(k * 256, (k + 1) * 256)
        later = sent_ref[4 * k : 4 * k + 4, :, :].reshape(256, STATE)
        back = mm(b, later, ((1,), (1,))) * mm(factors, spread[:, lanes], ((1,), (0,)))
        dx_ref[:, lanes] = (lead_ref[:, lanes].astype(F32) + back).astype(BF16)
        copy = pltpu.make_async_copy(
            dx_ref.at[:, pl.ds(k * 256, 256)],
            dx_out.at[0, 0, :, pl.ds(k * 256, 256)],
            sems.at[10 + k],
        )
        copy.start()
        copies.append(copy)
    for copy in copies:
        copy.wait()


def fold_kernel(fetch, got_ref, out_ref):
    flat = jnp.sum(got_ref[...], axis=0)
    for k in range(3):
        out_ref[k, :, :] = flat[:, k * HEADS : (k + 1) * HEADS]


def spread_out(value, axes):
    return lax.all_to_all(value, axes, 0, 0, tiled=True)


def relay(value):
    size = lax.axis_size("pipe")
    return lax.ppermute(value, "pipe", [(i, i - 1) for i in range(1, size)])


def layer(x, b, c, raw, log_row, bias_row, gain_row, g):
    x, b, c, raw, g = (v[0, 0] for v in (x, b, c, raw, g))
    raw = raw.T
    everyone = 1
    for name in DP_CTX:
        everyone *= lax.axis_size(name)
    pay, time = run_kernel(
        ends_kernel,
        (raw, log_row, bias_row, g, c, x, b),
        (),
        (shape((HEADS, 136, STATE), BF16), shape((2 * BLOCK, HEADS), F32)),
        (pltpu.VMEM((HEADS, 136, STATE), BF16), pltpu.SemaphoreType.DMA((2,))),
        far_outs=1,
    )
    got = spread_out(pay, CTX)
    lead, pack, acc, base, blank = run_kernel(
        inner_kernel,
        (x, g, b, c, raw, log_row, bias_row, gain_row),
        (time,),
        (
            shape((BLOCK, PACK), BF16),
            shape((BLOCK, 2 * WIDTH + 2 * STATE), BF16),
            shape((BLOCK, 2 * STATE + 8 * HEADS), F32),
            shape((BLOCK, WIDTH), F32),
            shape((everyone, 1, 128), F32),
        ),
        (pltpu.VMEM((BLOCK, WIDTH), F32), pltpu.VMEM((BLOCK, BLOCK), F32)),
    )
    lead = relay(lead)
    (states,) = run_kernel(
        join_kernel, (), (got, acc), (shape((RANKS, 128, STATE), BF16),)
    )
    states = spread_out(states, CTX)
    blank = pltpu.with_memory_space_constraint(blank, pltpu.HBM)
    par, sent = pl.pallas_call(
        outer_kernel,
        out_shape=(shape((everyone, 1, 128), F32), shape((SENT, HEAD_DIM, STATE), BF16)),
        in_specs=[ANY] + [VMEM] * 3,
        out_specs=(ANY, ANY),
        input_output_aliases={0: 0},
        scratch_shapes=[
            pltpu.VMEM((everyone, 1, 128), F32),
            pltpu.VMEM((9, HEAD_DIM, STATE), BF16),
            pltpu.SemaphoreType.DMA((3,)),
        ],
        interpret=INTERPRET,
        compiler_params=pltpu.CompilerParams(vmem_limit_bytes=24 * 1024 * 1024),
    )(blank, states, pack, acc)
    sent = relay(sent)
    par = spread_out(par, DP_CTX)
    (y,) = run_kernel(
        output_kernel,
        (),
        (states, pack, acc, base),
        (shape((1, 1, BLOCK, WIDTH), BF16),),
        grant=12,
    )
    dx, db, dc, draw = pl.pallas_call(
        received_kernel,
        out_shape=(
            shape((1, 1, BLOCK, WIDTH), BF16),
            shape((1, 1, BLOCK, STATE), BF16),
            shape((1, 1, BLOCK, STATE), BF16),
            shape((1, 1, HEADS, BLOCK), BF16),
        ),
        in_specs=[VMEM] * 2,
        out_specs=(ANY, ANY, ANY, ANY),
        scratch_shapes=[pltpu.VMEM((BLOCK, WIDTH), BF16), pltpu.SemaphoreType.DMA((14,))],
        interpret=INTERPRET,
        compiler_params=pltpu.CompilerParams(vmem_limit_bytes=6 * 1024 * 1024),
    )(lead, sent)
    (par,) = run_kernel(
        fold_kernel, (), (par,), (shape((3, 1, HEADS), F32),), grant=2
    )
    return y, dx, db, dc, jnp.swapaxes(draw, 2, 3), jnp.swapaxes(par, 0, 1)


def solution(mesh):
    finer = Mesh(
        mesh.devices.reshape(mesh.shape["dp"], mesh.shape["pipe"], mesh.shape["ctx"] // 2, 2),
        ("dp", "pipe", "ctx_0", "ctx_1"),
    )
    tokens = P("dp", "pipe", CTX, None)
    row = P("pipe", None)
    return jax.shard_map(
        layer,
        mesh=finer,
        in_specs=(tokens, tokens, tokens, tokens, row, row, row, tokens),
        out_specs=(tokens, tokens, tokens, tokens, tokens, P("pipe", None, None)),
        check_vma=False,
    )
```
